32 devices in a mesh: groups: 2 (over x), seq: 16 (over z, y, core).
Axes of the slice: x: 2, y: 2, z: 4, core: 2. Of those that a mesh axis runs over, the one named last changes fastest.
Arguments:
- features: bfloat16 [2, 2048, 640], P('groups', 'seq'), parts along dimension 0, may hold values from -18 to 18
- gain_first: float32 [640], replicated, may hold values from 0.1 to 1.9
- weight_first: bfloat16 [640, 3840], replicated, may hold values from -0.109375 to 0.109375
- gain_second: float32 [768], replicated, may hold values from 0.1 to 1.9
- weight_second: bfloat16 [768, 3840], replicated, may hold values from -0.09375 to 0.09375
- upstream: bfloat16 [2, 512, 768], P('groups', 'seq'), parts along dimension 0, may hold values from -4 to 4
Outputs:
- encoded: bfloat16 [2, 512, 768], P('groups', 'seq'), parts along dimension 0
- input_grad: bfloat16 [2, 2048, 640], P('groups', 'seq'), parts along dimension 0
- weight_first_grad: float32 [1280, 3840], P(('groups', 'seq')), parts along dimension 0
- weight_second_grad: float32 [1536, 3840], P(('groups', 'seq')), parts along dimension 0
- gain_first_grad: float32 [1280], P('groups'), parts along dimension 0
- gain_second_grad: float32 [1536], P('groups'), parts along dimension 0
The draws below stay inside these ranges and needn't reach their ends.
There are 2 independent parts, one for each index of `groups`. The reference program is written for one: setup_inputs(seed, part) draws one part's arguments, and reference() takes and returns one part's arrays. A program takes and returns all parts, laid end to end along the dimension named above; an argument that names none is the same for every part. Nothing has to cross between parts.
All inputs are finite; a program needn't handle non-finite values.
Results may differ from the reference program's by a relative error of at most 0.0053.
Values may be sent and summed in bfloat16 or wider, within the bound.
A program may use at most 128 MiB of HBM per device.

```python
import math
import jax
import jax.numpy as jnp
from jax import lax

C0 = 640
C1 = 768
C2 = 768
KERNEL = 5
SEQS = 1
L0 = 2048
L2 = 512


def draw_features(key, part):
    key_base, key_chan, key_pos = jax.random.split(key, 3)
    channel_scale = jnp.exp(jax.random.uniform(key_chan, (C0,), jnp.float32, math.log(0.3), math.log(3.0)))
    position_scale = jnp.exp(jax.random.uniform(key_pos, (SEQS, L0, 1), jnp.float32, math.log(0.5), math.log(1.5)))
    base = jnp.clip(jax.random.normal(key_base, (SEQS, L0, C0), jnp.float32), -4.0, 4.0)
    return (base * channel_scale * position_scale).astype(jnp.bfloat16)


def level_of(rng, dims, cuts, least, high):
    level = 1.0
    for position, blocks in cuts:
        heights = jax.random.uniform(jax.random.fold_in(jax.random.fold_in(rng, 6), position), (blocks,), jnp.float32, least / len(cuts), high / len(cuts))
        level = level * jnp.repeat(jnp.exp(heights), dims[position] // blocks).reshape((-1,) + (1,) * (len(dims) - 1 - position))
    return level


def noise(own_key, shape, scale, reach, cuts=(), kind=jnp.bfloat16):
    level = level_of(own_key, shape, cuts, -0.22, 0.18) if cuts else 1.0
    entries = jax.random.normal(own_key, shape, jnp.float32) * scale * level
    return jnp.minimum(jnp.maximum(entries, -reach), reach).astype(kind)


def setup_inputs(seed: int = 0, part: int = 0) -> dict:
    arg_keys = jax.random.split(jax.random.key(seed), 7)
    part_keys = jax.random.split(jax.random.fold_in(arg_keys[6], part), 7)
    return {
        "features": draw_features(jax.random.fold_in(jax.random.fold_in(arg_keys[6], part), 71), part),
        "gain_first": jnp.clip(1.0 + 0.18 * jax.random.normal(arg_keys[1], (C0,), jnp.float32), 0.1, 1.9),
        "weight_first": noise(arg_keys[2], (C0, KERNEL * C1), (KERNEL * C0) ** -0.5, 0.109375),
        "gain_second": jnp.clip(1.0 + 0.18 * jax.random.normal(arg_keys[3], (C1,), jnp.float32), 0.1, 1.9),
        "weight_second": noise(arg_keys[4], (C1, KERNEL * C2), (KERNEL * C1) ** -0.5, 0.09375),
        "upstream": noise(part_keys[5], (SEQS, L2, C2), 0.5, 4.0, ((1, 16),)),
    }


def norm_gelu(values, gain):
    floats = values.astype(jnp.float32)
    inverse = lax.rsqrt(lax.optimization_barrier(jnp.mean(floats * floats, axis=-1, keepdims=True)) + 1e-06)
    normed = floats * inverse * gain
    return (floats, normed, inverse, jax.nn.gelu(normed).astype(jnp.bfloat16))

def section_forward(values, gain, weight):
    chan_in = values.shape[-1]
    chan_out = weight.shape[1] // KERNEL
    length = values.shape[1]
    half_kernel = KERNEL // 2
    floats, normed, inverse, hidden = norm_gelu(values, gain)
    padded = jnp.pad(hidden, ((0, 0), (half_kernel, half_kernel), (0, 0)))
    conv_sum = jnp.zeros((values.shape[0], length, chan_out), jnp.float32)
    for k in range(KERNEL):
        conv_sum = conv_sum + jnp.dot(padded[:, k:k + length], weight[:, k * chan_out:(k + 1) * chan_out], preferred_element_type=jnp.float32)
    summed = conv_sum + jnp.pad(floats, ((0, 0), (0, 0), (0, chan_out - chan_in)))
    pooled = ((summed[:, 0::2] + summed[:, 1::2]) * 0.5).astype(jnp.bfloat16)
    return (pooled, (floats, normed, inverse, hidden))

def section_backward(upper, saved, gain, weight):
    floats, normed, inverse, hidden = saved
    chan_in = floats.shape[-1]
    chan_out = weight.shape[1] // KERNEL
    length = floats.shape[1]
    half_kernel = KERNEL // 2
    spread = jnp.repeat(upper, 2, axis=1) * 0.5
    padded = jnp.pad(spread, ((0, 0), (half_kernel, half_kernel), (0, 0)))
    back_acts = jnp.zeros((floats.shape[0], length, chan_in), jnp.float32)
    for k in range(KERNEL):
        offset = 2 * half_kernel - k
        back_acts = back_acts + jnp.dot(padded[:, offset:offset + length], weight[:, k * chan_out:(k + 1) * chan_out].T, preferred_element_type=jnp.float32)
    padded_hidden = jnp.pad(hidden, ((0, 0), (half_kernel, half_kernel), (0, 0)))
    spread_f = spread.astype(jnp.float32)
    blocks = []
    for k in range(KERNEL):
        blocks.append(jnp.einsum('blc,blo->co', padded_hidden[:, k:k + length].astype(jnp.float32), spread_f, precision=lax.Precision.HIGHEST))
    grad_weight = jnp.concatenate(blocks, axis=1)
    _, pullback = jax.vjp(jax.nn.gelu, normed)
    grad_norm = pullback(back_acts)[0]
    scaled = grad_norm * gain
    grad_gain = lax.optimization_barrier(jnp.sum(grad_norm * floats * inverse, axis=(0, 1)))
    grad_x = inverse * scaled - floats * inverse ** 3 * lax.optimization_barrier(jnp.mean(scaled * floats, axis=-1, keepdims=True)) + spread_f[:, :, :chan_in]
    return (grad_x.astype(jnp.bfloat16), grad_weight, grad_gain)

def reference(features, gain_first, weight_first, gain_second, weight_second, upstream):
    middle, saved_first = section_forward(features, gain_first, weight_first)
    encoded, saved_second = section_forward(middle, gain_second, weight_second)
    middle_grad, weight_second_grad, gain_second_grad = section_backward(upstream, saved_second, gain_second, weight_second)
    input_grad, weight_first_grad, gain_first_grad = section_backward(middle_grad, saved_first, gain_first, weight_first)
    return (encoded, input_grad, weight_first_grad, weight_second_grad, gain_first_grad, gain_second_grad)
```

```python
import functools
import jax
import jax.numpy as jnp
from jax import lax
from jax.experimental import pallas as pl
from jax.experimental.pallas import tpu as pltpu
from jax.sharding import PartitionSpec as P

KERNEL = 5
GELU_A = 0.7978845608028654
GELU_B = 0.044715
HALO = 8
F32 = jnp.float32
BF16 = jnp.bfloat16


def round16(rows):
    return (rows + 15) // 16 * 16


def dot(a, b):
    return jnp.dot(a, b, preferred_element_type=F32)


def dot_t(a, b):
    return lax.dot_general(a, b, (((1,), (1,)), ((), ())), preferred_element_type=F32)


def mean_inverse(x):
    return lax.rsqrt(jnp.mean(x * x, axis=-1, keepdims=True) + 1e-06)


def gelu(x):
    return 0.5 * x * (1.0 + jnp.tanh(GELU_A * (x + GELU_B * x * x * x)))


def gelu_slope(x):
    t = jnp.tanh(GELU_A * (x + GELU_B * x * x * x))
    return 0.5 * (1.0 + t) + 0.5 * x * (1.0 - t * t) * GELU_A * (1.0 + 3.0 * GELU_B * x * x)


def picks(shape, test, value):
    row = lax.broadcasted_iota(jnp.int32, shape, 0)
    col = lax.broadcasted_iota(jnp.int32, shape, 1)
    return jnp.where(test(row, col), value, 0.0).astype(BF16)


def kernel(
    n, x_ref, g1_ref, w1_hbm, g2_ref, w2_hbm, up_ref,
    enc_ref, dx_ref, dw1_ref, dw2_ref, dg1_ref, dg2_ref,
    w1_ref, w2_ref, xl_ref, xr_ref, ul_ref, ur_ref,
    cbuf, ubuf, asend, arecv, gbuf,
    w_sem, halo_send, halo_recv, c_send, c_recv, u_send, u_recv, a_send, a_recv, g_send, g_recv,
):
    me = lax.axis_index("seq")
    own1, c0 = x_ref.shape[0], x_ref.shape[1] // 2
    own2, c2 = up_ref.shape
    c1 = g2_ref.shape[1]
    ext1, ext2 = own1 + 2 * HALO, own2 + 2 * HALO
    rows1, rows2 = c0 // n, c1 // n
    pad1, pad2 = round16(rows1), round16(rows2)
    outer = n // 4
    core = lax.rem(me, 2)
    mid_axis = lax.rem(me // 2, 2)
    far = me // 4

    def peer_id(index):
        return {"seq": index}

    barrier = pltpu.get_barrier_semaphore()

    def greet(d, _):
        pl.semaphore_signal(barrier, inc=1, device_id=peer_id(lax.rem(me + d, n)), device_id_type=pl.DeviceIdType.MESH)
        return 0

    lax.fori_loop(1, n, greet, 0)
    w1_copy = pltpu.make_async_copy(w1_hbm, w1_ref, w_sem.at[0])
    w2_copy = pltpu.make_async_copy(w2_hbm, w2_ref, w_sem.at[1])
    w2_copy.start()
    w1_copy.start()
    ubuf[me] = up_ref[...]
    pl.semaphore_wait(barrier, n - 1)

    def remote(src, dst, send, recv, index):
        return pltpu.make_async_remote_copy(
            src_ref=src, dst_ref=dst, send_sem=send, recv_sem=recv,
            device_id=peer_id(index), device_id_type=pl.DeviceIdType.MESH,
        )

    left, right = lax.rem(me + n - 1, n), lax.rem(me + 1, n)
    x_to_right = remote(x_ref.at[pl.ds(own1 - 16, 16)], xl_ref, halo_send.at[0], halo_recv.at[0], right)
    x_to_left = remote(x_ref.at[pl.ds(0, 16)], xr_ref, halo_send.at[1], halo_recv.at[1], left)
    u_to_right = remote(up_ref.at[pl.ds(own2 - 16, 16)], ul_ref, halo_send.at[2], halo_recv.at[2], right)
    u_to_left = remote(up_ref.at[pl.ds(0, 16)], ur_ref, halo_send.at[3], halo_recv.at[3], left)

    @pl.when(me < n - 1)
    def _():
        x_to_right.start()
        u_to_right.start()

    @pl.when(me > 0)
    def _():
        x_to_left.start()
        u_to_left.start()

    def slot(f, m, c):
        return (f * 2 + m) * 2 + c

    def gather_parts(buf, send, recv):
        def push(owner, target, k):
            return remote(buf.at[owner], buf.at[owner], send.at[k], recv.at[owner], target)

        def arrive(owner):
            push(owner, right, 0).wait_recv()

        along = [lax.rem(far + d, outer) for d in range(outer)]
        back = [lax.rem(far + outer - d, outer) for d in range(outer)]
        across = slot(far, 1 - mid_axis, core)
        twin = slot(far, mid_axis, 1 - core)

        def begin():
            push(me, across, 0).start()
            for d in range(1, outer):
                push(me, slot(along[d], mid_axis, core), d).start()
            push(me, twin, outer).start()

        def relay_far():
            for d in range(1, outer):
                owner = slot(back[d], mid_axis, core)
                arrive(owner)
                push(owner, across, outer + d).start()
                push(owner, twin, 2 * outer - 1 + d).start()

        def relay_across():
            for d in range(outer):
                owner = slot(back[d], 1 - mid_axis, core)
                arrive(owner)
                push(owner, twin, 3 * outer - 1 + d).start()

        def finish():
            for d in range(outer):
                for m in range(2):
                    arrive(slot(back[d], m, 1 - core))

        def drain():
            for k in range(n - 1):
                push(me, right, k).wait_send()

        return begin, relay_far, relay_across, finish, drain

    u_begin, u_far, u_across, u_finish, u_drain = gather_parts(ubuf, u_send, u_recv)
    c_begin, c_far, c_across, c_finish, c_drain = gather_parts(cbuf, c_send, c_recv)
    u_begin()

    @pl.when(me == 0)
    def _():
        xl_ref[...] = jnp.zeros_like(xl_ref)
        ul_ref[...] = jnp.zeros_like(ul_ref)

    @pl.when(me == n - 1)
    def _():
        xr_ref[...] = jnp.zeros_like(xr_ref)
        ur_ref[...] = jnp.zeros_like(ur_ref)

    @pl.when(me > 0)
    def _():
        x_to_right.wait_recv()
        u_to_right.wait_recv()

    @pl.when(me < n - 1)
    def _():
        x_to_left.wait_recv()
        u_to_left.wait_recv()

    gain1, gain2 = g1_ref[...], g2_ref[...]
    x = jnp.concatenate(
        [xl_ref[...].astype(F32)[16 - HALO :], x_ref[...].astype(F32), xr_ref[...].astype(F32)[:HALO]], axis=0
    )

    def activate(part):
        r = mean_inverse(part)
        return r, gelu(part * r * gain1).astype(BF16).astype(F32)

    xe, xo = x[:, :c0], x[:, c0:]
    _, ue = activate(xe)
    _, uo = activate(xo)
    pairs = 0.5 * (ue + uo)
    cross = 0.5 * (pltpu.roll(uo, 1, 0) + ue)
    w2_copy.wait()
    up = jnp.concatenate(
        [ul_ref[...].astype(F32)[16 - HALO :], up_ref[...].astype(F32), ur_ref[...].astype(F32)[:HALO]], axis=0
    ).astype(BF16)
    du2 = jnp.zeros((ext1, c1), F32)
    spread = None
    for k in range(KERNEL):
        pick = picks(
            (ext1, ext2),
            lambda i, r: (2 * r == i + HALO + 2 - k) | (2 * r + 1 == i + HALO + 2 - k),
            0.5,
        )
        part = dot(pick, up)
        if k == KERNEL // 2:
            spread = part
        du2 = du2 + dot_t(part.astype(BF16), w2_ref[:, k * c2 : (k + 1) * c2])

    w1_copy.wait()
    sources = [pltpu.roll(pairs, 1, 0), cross, pairs, pltpu.roll(cross, ext1 - 1, 0), pltpu.roll(pairs, ext1 - 1, 0)]
    conv = jnp.zeros((ext1, c1), F32)
    for k in range(KERNEL):
        conv = conv + dot(sources[k].astype(BF16), w1_ref[:, k * c1 : (k + 1) * c1])
    held = 0.5 * (xe + xo)
    if c1 > c0:
        held = jnp.concatenate([held, jnp.zeros((ext1, c1 - c0), F32)], axis=1)
    place = me * own1 - HALO + lax.broadcasted_iota(jnp.int32, (ext1, 1), 0)
    inside = (place >= 0) & (place < n * own1)
    mid = jnp.where(inside, conv + held, 0.0).astype(BF16)
    midf = mid.astype(F32)
    r2 = mean_inverse(midf)
    n2 = midf * r2 * gain2
    u2 = gelu(n2).astype(BF16)
    dn2 = du2 * gelu_slope(n2)
    terms2 = dn2 * midf * r2
    dg2 = jnp.sum(terms2[HALO : HALO + own1], axis=0, keepdims=True)
    h2 = dn2 * gain2
    dmid = r2 * h2 - midf * (r2 * r2 * r2) * jnp.mean(h2 * midf, axis=-1, keepdims=True) + spread
    dmid = jnp.where(inside, dmid, 0.0)
    cbuf[me] = dmid[HALO : HALO + own1].astype(BF16)
    dmid = dmid.astype(BF16)
    c_begin()

    columns1 = jnp.concatenate([ue[HALO : HALO + own1], uo[HALO : HALO + own1]], axis=0).T
    order = picks(
        (128, ext1),
        lambda t, i: ((t < own2) & (i == 2 * t + HALO)) | ((t >= own2) & (t < 2 * own2) & (i == 2 * (t - own2) + HALO + 1)),
        1.0,
    )
    columns2 = dot(order, u2).T
    for s in range(n):
        first = columns1[s * rows1 : (s + 1) * rows1]
        second = columns2[s * rows2 : (s + 1) * rows2]
        if pad1 > rows1:
            first = jnp.concatenate([first, jnp.zeros((pad1 - rows1, 128), F32)], axis=0)
        if pad2 > rows2:
            second = jnp.concatenate([second, jnp.zeros((pad2 - rows2, 128), F32)], axis=0)
        asend[s, 0:pad1, :] = first.astype(BF16)
        asend[s, pad1 : pad1 + pad2, :] = second.astype(BF16)
    arecv[me] = asend[me]

    def a_copy(d):
        target = lax.rem(me + d, n)
        return remote(asend.at[target], arecv.at[me], a_send.at[d], a_recv.at[me], target)

    def a_start(d, _):
        a_copy(d).start()
        return 0

    lax.fori_loop(1, n, a_start, 0)

    u_far()
    back = [dot_t(dmid, w1_ref[:, k * c1 : (k + 1) * c1]) for k in range(KERNEL)]
    ahead = slice(HALO + 1, HALO + 1 + own1)
    here = slice(HALO, HALO + own1)
    behind = slice(HALO - 1, HALO - 1 + own1)
    du_even = 0.5 * (back[0][ahead] + (back[1] + back[2])[here] + (back[3] + back[4])[behind])
    du_odd = 0.5 * ((back[0] + back[1])[ahead] + (back[2] + back[3])[here] + back[4][behind])
    skip = 0.5 * dmid.astype(F32)[here, :c0]
    dg1 = jnp.zeros((1, c0), F32)
    for side, du in ((0, du_even), (1, du_odd)):
        xs = x_ref[:, side * c0 : (side + 1) * c0].astype(F32)
        r = mean_inverse(xs)
        dn = du * gelu_slope(xs * r * gain1)
        dg1 = dg1 + jnp.sum(dn * xs * r, axis=0, keepdims=True)
        h = dn * gain1
        dx = r * h - xs * (r * r * r) * jnp.mean(h * xs, axis=-1, keepdims=True) + skip
        dx_ref[:, side * c0 : (side + 1) * c0] = dx.astype(BF16)
    gbuf[me] = jnp.concatenate([dg1, dg2], axis=1)

    def g_copy(d):
        target = lax.rem(me + d, n)
        return remote(gbuf.at[me], gbuf.at[me], g_send.at[d], g_recv.at[me], target)

    def g_start(d, _):
        g_copy(d).start()
        return 0

    c_far()
    lax.fori_loop(1, n, g_start, 0)
    u_across()

    enc = jnp.zeros((own2, c2), F32)
    for k in range(KERNEL):
        taps = picks(
            (own2, ext1),
            lambda m, i: (i == 2 * m + k - 2 + HALO) | (i == 2 * m + k - 1 + HALO),
            0.5,
        )
        enc = enc + dot(dot(taps, u2).astype(BF16), w2_ref[:, k * c2 : (k + 1) * c2])
    halves = picks((own2, ext1), lambda m, i: (i == 2 * m + HALO) | (i == 2 * m + 1 + HALO), 0.5)
    pooled = dot(halves, mid)
    if c2 > c1:
        pooled = jnp.concatenate([pooled, jnp.zeros((own2, c2 - c1), F32)], axis=1)
    enc_ref[...] = (enc + pooled).astype(BF16)

    c_across()

    def a_done(d, _):
        source = lax.rem(me + n - d, n)
        remote(asend.at[source], arecv.at[source], a_send.at[d], a_recv.at[source], source).wait_recv()
        return 0

    lax.fori_loop(1, n, a_done, 0)

    def taps_of(start, rows, length):
        group = 128 // length
        lane = lax.broadcasted_iota(jnp.int32, (rows, 128), 1)
        evens, odds = [], []
        for s in range(0, n, group):
            even = odd = jnp.zeros((rows, 128), F32)
            for g in range(group):
                block = arecv[s + g, start : start + rows, :].astype(F32)
                chosen = (lane >= g * length) & (lane < (g + 1) * length)
                shift = g * length
                even = jnp.where(chosen, pltpu.roll(block, shift, 1) if shift else block, even)
                shift = (g * length - length) % 128
                odd = jnp.where(chosen, pltpu.roll(block, shift, 1) if shift else block, odd)
            evens.append(even)
            odds.append(odd)
        even = jnp.concatenate(evens, axis=1)
        odd = jnp.concatenate(odds, axis=1)
        total = n * length
        lanes = lax.broadcasted_iota(jnp.int32, (rows, total), 1)

        def later(v):
            return jnp.where(lanes == 0, 0.0, pltpu.roll(v, 1, 1))

        def sooner(v):
            return jnp.where(lanes == total - 1, 0.0, pltpu.roll(v, total - 1, 1))

        pair = 0.5 * (even + odd)
        blocks = [later(pair), 0.5 * (later(odd) + even), pair, 0.5 * (odd + sooner(even)), sooner(pair)]
        return jnp.concatenate(blocks, axis=0).astype(BF16)

    u_finish()
    stack2 = taps_of(pad1, pad2, own2)
    grad2 = dot(stack2, ubuf[...].reshape(n * own2, c2))
    for k in range(KERNEL):
        dw2_ref[:, k * c2 : (k + 1) * c2] = grad2[k * pad2 : k * pad2 + rows2]
    stack1 = taps_of(0, pad1, own1)

    def g_done(d, _):
        source = lax.rem(me + n - d, n)
        remote(gbuf.at[source], gbuf.at[source], g_send.at[d], g_recv.at[source], source).wait_recv()
        return 0

    lax.fori_loop(1, n, g_done, 0)
    gains = jnp.sum(gbuf[...], axis=0)
    dg1_ref[...] = gains[:, :c0]
    dg2_ref[...] = gains[:, c0:]
    c_finish()
    grad1 = dot(stack1, cbuf[...].reshape(n * own1, c1))
    for k in range(KERNEL):
        dw1_ref[:, k * c1 : (k + 1) * c1] = grad1[k * pad1 : k * pad1 + rows1]

    @pl.when(me < n - 1)
    def _():
        x_to_right.wait_send()
        u_to_right.wait_send()

    @pl.when(me > 0)
    def _():
        x_to_left.wait_send()
        u_to_left.wait_send()

    u_drain()
    c_drain()

    def drain(d, _):
        a_copy(d).wait_send()
        g_copy(d).wait_send()
        return 0

    lax.fori_loop(1, n, drain, 0)


def shards(features, gain_first, weight_first, gain_second, weight_second, upstream):
    n = lax.axis_size("seq")
    length, c0 = features.shape[1:]
    own2, c2 = upstream.shape[1:]
    c1 = weight_second.shape[0]
    own1 = length // 2
    pads = round16(c0 // n) + round16(c1 // n)
    dma = pltpu.SemaphoreType.DMA
    vmem = pl.BlockSpec(memory_space=pltpu.VMEM)
    hbm = pl.BlockSpec(memory_space=pl.ANY)
    encoded, dx, dw1, dw2, dg1, dg2 = pl.pallas_call(
        functools.partial(kernel, n),
        out_shape=(
            jax.ShapeDtypeStruct((own2, c2), BF16),
            jax.ShapeDtypeStruct((own1, 2 * c0), BF16),
            jax.ShapeDtypeStruct((c0 // n, KERNEL * c1), F32),
            jax.ShapeDtypeStruct((c1 // n, KERNEL * c2), F32),
            jax.ShapeDtypeStruct((1, c0), F32),
            jax.ShapeDtypeStruct((1, c1), F32),
        ),
        in_specs=[vmem, vmem, hbm, vmem, hbm, vmem],
        out_specs=(vmem,) * 6,
        scratch_shapes=[
            pltpu.VMEM(weight_first.shape, BF16),
            pltpu.VMEM(weight_second.shape, BF16),
            pltpu.VMEM((16, 2 * c0), BF16),
            pltpu.VMEM((16, 2 * c0), BF16),
            pltpu.VMEM((16, c2), BF16),
            pltpu.VMEM((16, c2), BF16),
            pltpu.VMEM((n, own1, c1), BF16),
            pltpu.VMEM((n, own2, c2), BF16),
            pltpu.VMEM((n, pads, 128), BF16),
            pltpu.VMEM((n, pads, 128), BF16),
            pltpu.VMEM((n, 1, c0 + c1), F32),
            dma((2,)), dma((4,)), dma((4,)),
            dma((n,)), dma((n,)), dma((n,)), dma((n,)), dma((n,)), dma((n,)), dma((n,)), dma((n,)),
        ],
        compiler_params=pltpu.CompilerParams(
            collective_id=0, has_side_effects=True, vmem_limit_bytes=56 * 1024 * 1024
        ),
    )(
        features.reshape(own1, 2 * c0),
        gain_first[None],
        weight_first,
        gain_second[None],
        weight_second,
        upstream[0],
    )
    return (encoded[None], dx.reshape(1, length, c0), dw1, dw2, dg1[0], dg2[0])


def solution(mesh):
    placed = (P("groups", "seq", None), P(), P(), P(), P(), P("groups", "seq", None))
    return jax.shard_map(
        shards,
        mesh=mesh,
        in_specs=placed,
        out_specs=(
            P("groups", "seq", None),
            P("groups", "seq", None),
            P(("groups", "seq"), None),
            P(("groups", "seq"), None),
            P("groups"),
            P("groups"),
        ),
        check_vma=False,
    )
```

```python
import functools
import jax
import jax.numpy as jnp
from jax import lax
from jax.experimental import pallas as pl
from jax.experimental.pallas import tpu as pltpu
from jax.sharding import PartitionSpec as P

KERNEL = 5
GELU_A = 0.7978845608028654
GELU_B = 0.044715
HALO = 8
F32 = jnp.float32
BF16 = jnp.bfloat16


def round16(rows):
    return (rows + 15) // 16 * 16


def dot(a, b):
    return jnp.dot(a, b, preferred_element_type=F32)


def dot_t(a, b):
    return lax.dot_general(a, b, (((1,), (1,)), ((), ())), preferred_element_type=F32)


def mean_inverse(x):
    return lax.rsqrt(jnp.mean(x * x, axis=-1, keepdims=True) + 1e-06)


def gelu(x):
    return 0.5 * x * (1.0 + jnp.tanh(GELU_A * (x + GELU_B * x * x * x)))


def gelu_slope(x):
    t = jnp.tanh(GELU_A * (x + GELU_B * x * x * x))
    return 0.5 * (1.0 + t) + 0.5 * x * (1.0 - t * t) * GELU_A * (1.0 + 3.0 * GELU_B * x * x)


def picks(shape, test, value):
    row = lax.broadcasted_iota(jnp.int32, shape, 0)
    col = lax.broadcasted_iota(jnp.int32, shape, 1)
    return jnp.where(test(row, col), value, 0.0).astype(BF16)


def kernel(
    n, x_ref, g1_ref, w1_hbm, g2_ref, w2_hbm, up_ref,
    enc_ref, dx_ref, dw1_ref, dw2_ref, dg1_ref, dg2_ref,
    w1_ref, w2_ref, xl_ref, xr_ref, ul_ref, ur_ref,
    cbuf, ubuf, asend, arecv, gbuf,
    w_sem, halo_send, halo_recv, c_send, c_recv, u_send, u_recv, a_send, a_recv, g_send, g_recv,
):
    me = lax.axis_index("seq")
    own1, c0 = x_ref.shape[1] // 2, x_ref.shape[2]
    own2, c2 = up_ref.shape[1:]
    c1 = g2_ref.shape[0]
    ext1, ext2 = own1 + 2 * HALO, own2 + 2 * HALO
    rows1, rows2 = c0 // n, c1 // n
    pad1, pad2 = round16(rows1), round16(rows2)
    outer = n // 4
    core = lax.rem(me, 2)
    mid_axis = lax.rem(me // 2, 2)
    far = me // 4

    def peer_id(index):
        return {"seq": index}

    barrier = pltpu.get_barrier_semaphore()

    def greet(d, _):
        pl.semaphore_signal(barrier, inc=1, device_id=peer_id(lax.rem(me + d, n)), device_id_type=pl.DeviceIdType.MESH)
        return 0

    lax.fori_loop(1, n, greet, 0)
    w1_copy = pltpu.make_async_copy(w1_hbm, w1_ref, w_sem.at[0])
    w2_copy = pltpu.make_async_copy(w2_hbm, w2_ref, w_sem.at[1])
    w2_copy.start()
    w1_copy.start()
    ubuf[me] = up_ref[0]
    pl.semaphore_wait(barrier, n - 1)

    def remote(src, dst, send, recv, index):
        return pltpu.make_async_remote_copy(
            src_ref=src, dst_ref=dst, send_sem=send, recv_sem=recv,
            device_id=peer_id(index), device_id_type=pl.DeviceIdType.MESH,
        )

    left, right = lax.rem(me + n - 1, n), lax.rem(me + 1, n)
    x_to_right = remote(x_ref.at[0, pl.ds(2 * own1 - 16, 16)], xl_ref, halo_send.at[0], halo_recv.at[0], right)
    x_to_left = remote(x_ref.at[0, pl.ds(0, 16)], xr_ref, halo_send.at[1], halo_recv.at[1], left)
    u_to_right = remote(up_ref.at[0, pl.ds(own2 - 16, 16)], ul_ref, halo_send.at[2], halo_recv.at[2], right)
    u_to_left = remote(up_ref.at[0, pl.ds(0, 16)], ur_ref, halo_send.at[3], halo_recv.at[3], left)

    @pl.when(me < n - 1)
    def _():
        x_to_right.start()
        u_to_right.start()

    @pl.when(me > 0)
    def _():
        x_to_left.start()
        u_to_left.start()

    def slot(f, m, c):
        return (f * 2 + m) * 2 + c

    def gather_parts(buf, send, recv):
        def push(owner, target, k):
            return remote(buf.at[owner], buf.at[owner], send.at[k], recv.at[owner], target)

        def arrive(owner):
            push(owner, right, 0).wait_recv()

        along = [lax.rem(far + d, outer) for d in range(outer)]
        back = [lax.rem(far + outer - d, outer) for d in range(outer)]
        across = slot(far, 1 - mid_axis, core)
        twin = slot(far, mid_axis, 1 - core)

        def begin():
            push(me, across, 0).start()
            for d in range(1, outer):
                push(me, slot(along[d], mid_axis, core), d).start()
            push(me, twin, outer).start()

        def relay_far():
            for d in range(1, outer):
                owner = slot(back[d], mid_axis, core)
                arrive(owner)
                push(owner, across, outer + d).start()
                push(owner, twin, 2 * outer - 1 + d).start()

        def relay_across():
            for d in range(outer):
                owner = slot(back[d], 1 - mid_axis, core)
                arrive(owner)
                push(owner, twin, 3 * outer - 1 + d).start()

        def finish():
            for d in range(outer):
                for m in range(2):
                    arrive(slot(back[d], m, 1 - core))

        def drain():
            for k in range(n - 1):
                push(me, right, k).wait_send()

        return begin, relay_far, relay_across, finish, drain

    u_begin, u_far, u_across, u_finish, u_drain = gather_parts(ubuf, u_send, u_recv)
    c_begin, c_far, c_across, c_finish, c_drain = gather_parts(cbuf, c_send, c_recv)
    u_begin()

    @pl.when(me == 0)
    def _():
        xl_ref[...] = jnp.zeros_like(xl_ref)
        ul_ref[...] = jnp.zeros_like(ul_ref)

    @pl.when(me == n - 1)
    def _():
        xr_ref[...] = jnp.zeros_like(xr_ref)
        ur_ref[...] = jnp.zeros_like(ur_ref)

    @pl.when(me > 0)
    def _():
        x_to_right.wait_recv()
        u_to_right.wait_recv()

    @pl.when(me < n - 1)
    def _():
        x_to_left.wait_recv()
        u_to_left.wait_recv()

    gain1, gain2 = g1_ref[...].reshape(1, c0), g2_ref[...].reshape(1, c1)
    x = jnp.concatenate([xl_ref[...], x_ref[0], xr_ref[...]], axis=0)

    def activate(part):
        r = mean_inverse(part)
        return r, gelu(part * r * gain1).astype(BF16).astype(F32)

    xe = dot(picks((ext1, 2 * ext1), lambda j, i: i == 2 * j, 1.0), x)
    xo = dot(picks((ext1, 2 * ext1), lambda j, i: i == 2 * j + 1, 1.0), x)
    _, ue = activate(xe)
    _, uo = activate(xo)
    pairs = 0.5 * (ue + uo)
    cross = 0.5 * (pltpu.roll(uo, 1, 0) + ue)
    w2_copy.wait()
    up = jnp.concatenate(
        [ul_ref[...].astype(F32)[16 - HALO :], up_ref[0].astype(F32), ur_ref[...].astype(F32)[:HALO]], axis=0
    ).astype(BF16)
    du2 = jnp.zeros((ext1, c1), F32)
    spread = None
    for k in range(KERNEL):
        pick = picks(
            (ext1, ext2),
            lambda i, r: (2 * r == i + HALO + 2 - k) | (2 * r + 1 == i + HALO + 2 - k),
            0.5,
        )
        part = dot(pick, up)
        if k == KERNEL // 2:
            spread = part
        du2 = du2 + dot_t(part.astype(BF16), w2_ref[:, k * c2 : (k + 1) * c2])

    w1_copy.wait()
    sources = [pltpu.roll(pairs, 1, 0), cross, pairs, pltpu.roll(cross, ext1 - 1, 0), pltpu.roll(pairs, ext1 - 1, 0)]
    conv = jnp.zeros((ext1, c1), F32)
    for k in range(KERNEL):
        conv = conv + dot(sources[k].astype(BF16), w1_ref[:, k * c1 : (k + 1) * c1])
    held = 0.5 * (xe + xo)
    if c1 > c0:
        held = jnp.concatenate([held, jnp.zeros((ext1, c1 - c0), F32)], axis=1)
    place = me * own1 - HALO + lax.broadcasted_iota(jnp.int32, (ext1, 1), 0)
    inside = (place >= 0) & (place < n * own1)
    mid = jnp.where(inside, conv + held, 0.0).astype(BF16)
    midf = mid.astype(F32)
    r2 = mean_inverse(midf)
    n2 = midf * r2 * gain2
    u2 = gelu(n2).astype(BF16)
    dn2 = du2 * gelu_slope(n2)
    terms2 = dn2 * midf * r2
    dg2 = jnp.sum(terms2[HALO : HALO + own1], axis=0, keepdims=True)
    h2 = dn2 * gain2
    dmid = r2 * h2 - midf * (r2 * r2 * r2) * jnp.mean(h2 * midf, axis=-1, keepdims=True) + spread
    dmid = jnp.where(inside, dmid, 0.0)
    cbuf[me] = dmid[HALO : HALO + own1].astype(BF16)
    dmid = dmid.astype(BF16)
    c_begin()

    columns1 = jnp.concatenate([ue[HALO : HALO + own1], uo[HALO : HALO + own1]], axis=0).T
    order = picks(
        (128, ext1),
        lambda t, i: ((t < own2) & (i == 2 * t + HALO)) | ((t >= own2) & (t < 2 * own2) & (i == 2 * (t - own2) + HALO + 1)),
        1.0,
    )
    columns2 = dot(order, u2).T
    for s in range(n):
        first = columns1[s * rows1 : (s + 1) * rows1]
        second = columns2[s * rows2 : (s + 1) * rows2]
        if pad1 > rows1:
            first = jnp.concatenate([first, jnp.zeros((pad1 - rows1, 128), F32)], axis=0)
        if pad2 > rows2:
            second = jnp.concatenate([second, jnp.zeros((pad2 - rows2, 128), F32)], axis=0)
        asend[s, 0:pad1, :] = first.astype(BF16)
        asend[s, pad1 : pad1 + pad2, :] = second.astype(BF16)
    arecv[me] = asend[me]

    def a_copy(d):
        target = lax.rem(me + d, n)
        return remote(asend.at[target], arecv.at[me], a_send.at[d], a_recv.at[me], target)

    def a_start(d, _):
        a_copy(d).start()
        return 0

    lax.fori_loop(1, n, a_start, 0)

    u_far()
    back = [dot_t(dmid, w1_ref[:, k * c1 : (k + 1) * c1]) for k in range(KERNEL)]
    ahead = slice(HALO + 1, HALO + 1 + own1)
    here = slice(HALO, HALO + own1)
    behind = slice(HALO - 1, HALO - 1 + own1)
    du_even = 0.5 * (back[0][ahead] + (back[1] + back[2])[here] + (back[3] + back[4])[behind])
    du_odd = 0.5 * ((back[0] + back[1])[ahead] + (back[2] + back[3])[here] + back[4][behind])
    skip = 0.5 * dmid.astype(F32)[here, :c0]
    dg1 = jnp.zeros((1, c0), F32)
    sides = []
    for ext, du in ((xe, du_even), (xo, du_odd)):
        xs = ext[here]
        r = mean_inverse(xs)
        dn = du * gelu_slope(xs * r * gain1)
        dg1 = dg1 + jnp.sum(dn * xs * r, axis=0, keepdims=True)
        h = dn * gain1
        dx = r * h - xs * (r * r * r) * jnp.mean(h * xs, axis=-1, keepdims=True) + skip
        sides.append(dx.astype(BF16))
    weave_even = picks((2 * own1, own1), lambda i, j: i == 2 * j, 1.0)
    weave_odd = picks((2 * own1, own1), lambda i, j: i == 2 * j + 1, 1.0)
    dx_ref[0] = (dot(weave_even, sides[0]) + dot(weave_odd, sides[1])).astype(BF16)
    gbuf[me] = jnp.concatenate([dg1, dg2], axis=1)

    def g_copy(d):
        target = lax.rem(me + d, n)
        return remote(gbuf.at[me], gbuf.at[me], g_send.at[d], g_recv.at[me], target)

    def g_start(d, _):
        g_copy(d).start()
        return 0

    c_far()
    lax.fori_loop(1, n, g_start, 0)
    u_across()

    enc = jnp.zeros((own2, c2), F32)
    for k in range(KERNEL):
        taps = picks(
            (own2, ext1),
            lambda m, i: (i == 2 * m + k - 2 + HALO) | (i == 2 * m + k - 1 + HALO),
            0.5,
        )
        enc = enc + dot(dot(taps, u2).astype(BF16), w2_ref[:, k * c2 : (k + 1) * c2])
    halves = picks((own2, ext1), lambda m, i: (i == 2 * m + HALO) | (i == 2 * m + 1 + HALO), 0.5)
    pooled = dot(halves, mid)
    if c2 > c1:
        pooled = jnp.concatenate([pooled, jnp.zeros((own2, c2 - c1), F32)], axis=1)
    enc_ref[0] = (enc + pooled).astype(BF16)

    c_across()

    def a_done(d, _):
        source = lax.rem(me + n - d, n)
        remote(asend.at[source], arecv.at[source], a_send.at[d], a_recv.at[source], source).wait_recv()
        return 0

    lax.fori_loop(1, n, a_done, 0)

    def taps_of(start, rows, length):
        group = 128 // length
        lane = lax.broadcasted_iota(jnp.int32, (rows, 128), 1)
        evens, odds = [], []
        for s in range(0, n, group):
            even = odd = jnp.zeros((rows, 128), F32)
            for g in range(group):
                block = arecv[s + g, start : start + rows, :].astype(F32)
                chosen = (lane >= g * length) & (lane < (g + 1) * length)
                shift = g * length
                even = jnp.where(chosen, pltpu.roll(block, shift, 1) if shift else block, even)
                shift = (g * length - length) % 128
                odd = jnp.where(chosen, pltpu.roll(block, shift, 1) if shift else block, odd)
            evens.append(even)
            odds.append(odd)
        even = jnp.concatenate(evens, axis=1)
        odd = jnp.concatenate(odds, axis=1)
        total = n * length
        lanes = lax.broadcasted_iota(jnp.int32, (rows, total), 1)

        def later(v):
            return jnp.where(lanes == 0, 0.0, pltpu.roll(v, 1, 1))

        def sooner(v):
            return jnp.where(lanes == total - 1, 0.0, pltpu.roll(v, total - 1, 1))

        pair = 0.5 * (even + odd)
        blocks = [later(pair), 0.5 * (later(odd) + even), pair, 0.5 * (odd + sooner(even)), sooner(pair)]
        return jnp.concatenate(blocks, axis=0).astype(BF16)

    u_finish()
    stack2 = taps_of(pad1, pad2, own2)
    grad2 = dot(stack2, ubuf[...].reshape(n * own2, c2))
    for k in range(KERNEL):
        dw2_ref[:, k * c2 : (k + 1) * c2] = grad2[k * pad2 : k * pad2 + rows2]
    stack1 = taps_of(0, pad1, own1)

    def g_done(d, _):
        source = lax.rem(me + n - d, n)
        remote(gbuf.at[source], gbuf.at[source], g_send.at[d], g_recv.at[source], source).wait_recv()
        return 0

    lax.fori_loop(1, n, g_done, 0)
    gains = jnp.sum(gbuf[...], axis=0)
    dg1_ref[...] = gains[:, :c0].reshape(c0)
    dg2_ref[...] = gains[:, c0:].reshape(c1)
    c_finish()
    grad1 = dot(stack1, cbuf[...].reshape(n * own1, c1))
    for k in range(KERNEL):
        dw1_ref[:, k * c1 : (k + 1) * c1] = grad1[k * pad1 : k * pad1 + rows1]

    @pl.when(me < n - 1)
    def _():
        x_to_right.wait_send()
        u_to_right.wait_send()

    @pl.when(me > 0)
    def _():
        x_to_left.wait_send()
        u_to_left.wait_send()

    u_drain()
    c_drain()

    def drain(d, _):
        a_copy(d).wait_send()
        g_copy(d).wait_send()
        return 0

    lax.fori_loop(1, n, drain, 0)


def place_results(*refs):
    count = len(refs) // 2
    sems = refs[-1]
    copies = [pltpu.make_async_copy(refs[i], refs[count + i], sems.at[i]) for i in range(count)]
    for copy in copies:
        copy.start()
    for copy in copies:
        copy.wait()


def shards(features, gain_first, weight_first, gain_second, weight_second, upstream):
    n = lax.axis_size("seq")
    length, c0 = features.shape[1:]
    own2, c2 = upstream.shape[1:]
    c1 = weight_second.shape[0]
    own1 = length // 2
    pads = round16(c0 // n) + round16(c1 // n)
    dma = pltpu.SemaphoreType.DMA
    vmem = pl.BlockSpec(memory_space=pltpu.VMEM)
    hbm = pl.BlockSpec(memory_space=pl.ANY)
    results = pl.pallas_call(
        functools.partial(kernel, n),
        out_shape=(
            jax.ShapeDtypeStruct((1, own2, c2), BF16),
            jax.ShapeDtypeStruct((1, length, c0), BF16),
            jax.ShapeDtypeStruct((c0 // n, KERNEL * c1), F32),
            jax.ShapeDtypeStruct((c1 // n, KERNEL * c2), F32),
            jax.ShapeDtypeStruct((c0,), F32),
            jax.ShapeDtypeStruct((c1,), F32),
        ),
        in_specs=[vmem, vmem, hbm, vmem, hbm, vmem],
        out_specs=(vmem,) * 6,
        scratch_shapes=[
            pltpu.VMEM(weight_first.shape, BF16),
            pltpu.VMEM(weight_second.shape, BF16),
            pltpu.VMEM((16, c0), BF16),
            pltpu.VMEM((16, c0), BF16),
            pltpu.VMEM((16, c2), BF16),
            pltpu.VMEM((16, c2), BF16),
            pltpu.VMEM((n, own1, c1), BF16),
            pltpu.VMEM((n, own2, c2), BF16),
            pltpu.VMEM((n, pads, 128), BF16),
            pltpu.VMEM((n, pads, 128), BF16),
            pltpu.VMEM((n, 1, c0 + c1), F32),
            dma((2,)), dma((4,)), dma((4,)),
            dma((n,)), dma((n,)), dma((n,)), dma((n,)), dma((n,)), dma((n,)), dma((n,)), dma((n,)),
        ],
        compiler_params=pltpu.CompilerParams(
            collective_id=0, has_side_effects=True, vmem_limit_bytes=56 * 1024 * 1024
        ),
    )(
        features,
        gain_first,
        weight_first,
        gain_second,
        weight_second,
        upstream,
    )
    return pl.pallas_call(
        place_results,
        out_shape=tuple(jax.ShapeDtypeStruct(r.shape, r.dtype) for r in results),
        in_specs=[hbm] * len(results),
        out_specs=(hbm,) * len(results),
        scratch_shapes=[dma((len(results),))],
    )(*results)


def solution(mesh):
    placed = (P("groups", "seq", None), P(), P(), P(), P(), P("groups", "seq", None))
    return jax.shard_map(
        shards,
        mesh=mesh,
        in_specs=placed,
        out_specs=(
            P("groups", "seq", None),
            P("groups", "seq", None),
            P(("groups", "seq"), None),
            P(("groups", "seq"), None),
            P("groups"),
            P("groups"),
        ),
        check_vma=False,
    )
```

```python
import functools
import jax
import jax.numpy as jnp
from jax import lax
from jax.experimental import pallas as pl
from jax.experimental.pallas import tpu as pltpu
from jax.sharding import PartitionSpec as P

KERNEL = 5
GELU_A = 0.7978845608028654
GELU_B = 0.044715
HALO = 8
F32 = jnp.float32
BF16 = jnp.bfloat16


def round16(rows):
    return (rows + 15) // 16 * 16


def dot(a, b):
    return jnp.dot(a, b, preferred_element_type=F32)


def dot_t(a, b):
    return lax.dot_general(a, b, (((1,), (1,)), ((), ())), preferred_element_type=F32)


def mean_inverse(x):
    return lax.rsqrt(jnp.mean(x * x, axis=-1, keepdims=True) + 1e-06)


def gelu(x):
    return 0.5 * x * (1.0 + jnp.tanh(GELU_A * (x + GELU_B * x * x * x)))


def gelu_slope(x):
    t = jnp.tanh(GELU_A * (x + GELU_B * x * x * x))
    return 0.5 * (1.0 + t) + 0.5 * x * (1.0 - t * t) * GELU_A * (1.0 + 3.0 * GELU_B * x * x)


def picks(shape, test, value):
    row = lax.broadcasted_iota(jnp.int32, shape, 0)
    col = lax.broadcasted_iota(jnp.int32, shape, 1)
    return jnp.where(test(row, col), value, 0.0).astype(BF16)


def kernel(
    n, x_ref, g1_ref, w1_hbm, g2_ref, w2_hbm, up_ref,
    enc_ref, dx_ref, dw1_ref, dw2_ref, dg1_ref, dg2_ref,
    w1_ref, w2_ref, xl_ref, xr_ref, ul_ref, ur_ref,
    cbuf, ubuf, asend1, arecv1, asend2, arecv2, gbuf,
    w_sem, halo_send, halo_recv, c_send, c_recv, u_send, u_recv, a_send, a_recv, b_send, b_recv, g_send, g_recv,
):
    me = lax.axis_index("seq")
    own1, c0 = x_ref.shape[1] // 2, x_ref.shape[2]
    own2, c2 = up_ref.shape[1:]
    c1 = g2_ref.shape[0]
    ext1, ext2 = own1 + 2 * HALO, own2 + 2 * HALO
    rows1, rows2 = c0 // n, c1 // n
    pad1, pad2 = round16(rows1), round16(rows2)
    outer = n // 4
    core = lax.rem(me, 2)
    mid_axis = lax.rem(me // 2, 2)
    far = me // 4

    def peer_id(index):
        return {"seq": index}

    barrier = pltpu.get_barrier_semaphore()

    def greet(d, _):
        pl.semaphore_signal(barrier, inc=1, device_id=peer_id(lax.rem(me + d, n)), device_id_type=pl.DeviceIdType.MESH)
        return 0

    lax.fori_loop(1, n, greet, 0)
    w1_copy = pltpu.make_async_copy(w1_hbm, w1_ref, w_sem.at[0])
    w2_copy = pltpu.make_async_copy(w2_hbm, w2_ref, w_sem.at[1])
    w2_copy.start()
    w1_copy.start()
    ubuf[me] = up_ref[0]
    pl.semaphore_wait(barrier, n - 1)

    def remote(src, dst, send, recv, index):
        return pltpu.make_async_remote_copy(
            src_ref=src, dst_ref=dst, send_sem=send, recv_sem=recv,
            device_id=peer_id(index), device_id_type=pl.DeviceIdType.MESH,
        )

    left, right = lax.rem(me + n - 1, n), lax.rem(me + 1, n)
    x_to_right = remote(x_ref.at[0, pl.ds(2 * own1 - 16, 16)], xl_ref, halo_send.at[0], halo_recv.at[0], right)
    x_to_left = remote(x_ref.at[0, pl.ds(0, 16)], xr_ref, halo_send.at[1], halo_recv.at[1], left)
    u_to_right = remote(up_ref.at[0, pl.ds(own2 - 16, 16)], ul_ref, halo_send.at[2], halo_recv.at[2], right)
    u_to_left = remote(up_ref.at[0, pl.ds(0, 16)], ur_ref, halo_send.at[3], halo_recv.at[3], left)

    @pl.when(me < n - 1)
    def _():
        x_to_right.start()
        u_to_right.start()

    @pl.when(me > 0)
    def _():
        x_to_left.start()
        u_to_left.start()

    def slot(f, m, c):
        return (f * 2 + m) * 2 + c

    def gather_parts(buf, send, recv):
        def push(owner, target, k):
            return remote(buf.at[owner], buf.at[owner], send.at[k], recv.at[owner], target)

        def arrive(owner):
            push(owner, right, 0).wait_recv()

        along = [lax.rem(far + d, outer) for d in range(outer)]
        back = [lax.rem(far + outer - d, outer) for d in range(outer)]
        across = slot(far, 1 - mid_axis, core)
        twin = slot(far, mid_axis, 1 - core)

        def begin():
            push(me, across, 0).start()
            for d in range(1, outer):
                push(me, slot(along[d], mid_axis, core), d).start()
            push(me, twin, outer).start()

        def relay_far():
            for d in range(1, outer):
                owner = slot(back[d], mid_axis, core)
                arrive(owner)
                push(owner, across, outer + d).start()
                push(owner, twin, 2 * outer - 1 + d).start()

        def relay_across():
            for d in range(outer):
                owner = slot(back[d], 1 - mid_axis, core)
                arrive(owner)
                push(owner, twin, 3 * outer - 1 + d).start()

        def finish():
            for d in range(outer):
                for m in range(2):
                    arrive(slot(back[d], m, 1 - core))

        def drain():
            for k in range(n - 1):
                push(me, right, k).wait_send()

        return begin, relay_far, relay_across, finish, drain

    u_begin, u_far, u_across, u_finish, u_drain = gather_parts(ubuf, u_send, u_recv)
    c_begin, c_far, c_across, c_finish, c_drain = gather_parts(cbuf, c_send, c_recv)
    u_begin()

    @pl.when(me == 0)
    def _():
        xl_ref[...] = jnp.zeros_like(xl_ref)
        ul_ref[...] = jnp.zeros_like(ul_ref)

    @pl.when(me == n - 1)
    def _():
        xr_ref[...] = jnp.zeros_like(xr_ref)
        ur_ref[...] = jnp.zeros_like(ur_ref)

    @pl.when(me > 0)
    def _():
        x_to_right.wait_recv()
        u_to_right.wait_recv()

    @pl.when(me < n - 1)
    def _():
        x_to_left.wait_recv()
        u_to_left.wait_recv()

    gain1, gain2 = g1_ref[...].reshape(1, c0), g2_ref[...].reshape(1, c1)
    x = jnp.concatenate([xl_ref[...], x_ref[0], xr_ref[...]], axis=0)

    def activate(part):
        r = mean_inverse(part)
        return r, gelu(part * r * gain1).astype(BF16).astype(F32)

    xe = dot(picks((ext1, 2 * ext1), lambda j, i: i == 2 * j, 1.0), x)
    xo = dot(picks((ext1, 2 * ext1), lambda j, i: i == 2 * j + 1, 1.0), x)
    _, ue = activate(xe)
    _, uo = activate(xo)
    pairs = 0.5 * (ue + uo)
    cross = 0.5 * (pltpu.roll(uo, 1, 0) + ue)
    columns1 = jnp.concatenate([ue[HALO : HALO + own1], uo[HALO : HALO + own1]], axis=0).T
    for s in range(n):
        asend1[s] = columns1[s * rows1 : (s + 1) * rows1].astype(BF16)
    arecv1[me] = asend1[me]

    def exchange(sent, received, send, recv):
        def copy(d):
            target = lax.rem(me + d, n)
            return remote(sent.at[target], received.at[me], send.at[d], recv.at[me], target)

        def start(d, _):
            copy(d).start()
            return 0

        def arrive(d, _):
            source = lax.rem(me + n - d, n)
            remote(sent.at[source], received.at[source], send.at[d], recv.at[source], source).wait_recv()
            return 0

        return copy, start, arrive

    a_copy, a_start, a_done = exchange(asend1, arecv1, a_send, a_recv)
    b_copy, b_start, b_done = exchange(asend2, arecv2, b_send, b_recv)
    lax.fori_loop(1, n, a_start, 0)
    w2_copy.wait()
    up = jnp.concatenate(
        [ul_ref[...].astype(F32)[16 - HALO :], up_ref[0].astype(F32), ur_ref[...].astype(F32)[:HALO]], axis=0
    ).astype(BF16)
    du2 = jnp.zeros((ext1, c1), F32)
    spread = None
    for k in range(KERNEL):
        pick = picks(
            (ext1, ext2),
            lambda i, r: (2 * r == i + HALO + 2 - k) | (2 * r + 1 == i + HALO + 2 - k),
            0.5,
        )
        part = dot(pick, up)
        if k == KERNEL // 2:
            spread = part
        du2 = du2 + dot_t(part.astype(BF16), w2_ref[:, k * c2 : (k + 1) * c2])

    u_far()
    w1_copy.wait()
    sources = [pltpu.roll(pairs, 1, 0), cross, pairs, pltpu.roll(cross, ext1 - 1, 0), pltpu.roll(pairs, ext1 - 1, 0)]
    conv = jnp.zeros((ext1, c1), F32)
    for k in range(KERNEL):
        conv = conv + dot(sources[k].astype(BF16), w1_ref[:, k * c1 : (k + 1) * c1])
    u_across()
    held = 0.5 * (xe + xo)
    if c1 > c0:
        held = jnp.concatenate([held, jnp.zeros((ext1, c1 - c0), F32)], axis=1)
    place = me * own1 - HALO + lax.broadcasted_iota(jnp.int32, (ext1, 1), 0)
    inside = (place >= 0) & (place < n * own1)
    mid = jnp.where(inside, conv + held, 0.0).astype(BF16)
    midf = mid.astype(F32)
    r2 = mean_inverse(midf)
    n2 = midf * r2 * gain2
    u2 = gelu(n2).astype(BF16)
    dn2 = du2 * gelu_slope(n2)
    terms2 = dn2 * midf * r2
    dg2 = jnp.sum(terms2[HALO : HALO + own1], axis=0, keepdims=True)
    h2 = dn2 * gain2
    dmid = r2 * h2 - midf * (r2 * r2 * r2) * jnp.mean(h2 * midf, axis=-1, keepdims=True) + spread
    dmid = jnp.where(inside, dmid, 0.0)
    cbuf[me] = dmid[HALO : HALO + own1].astype(BF16)
    dmid = dmid.astype(BF16)
    c_begin()

    order = picks(
        (128, ext1),
        lambda t, i: ((t % 64 < own2) & (i == 2 * (t % 64) + HALO))
        | ((t % 64 >= own2) & (i == 2 * (t % 64 - own2) + HALO + 1)),
        1.0,
    )
    columns2 = dot(order, u2).T
    low = lax.broadcasted_iota(jnp.int32, (rows2 // 2, 128), 1) < 64
    for s in range(n):
        top = columns2[s * rows2 : s * rows2 + rows2 // 2]
        bottom = columns2[s * rows2 + rows2 // 2 : (s + 1) * rows2]
        asend2[s] = jnp.where(low, top, bottom).astype(BF16)
    arecv2[me] = asend2[me]
    lax.fori_loop(1, n, b_start, 0)

    back = [dot_t(dmid, w1_ref[:, k * c1 : (k + 1) * c1]) for k in range(KERNEL)]
    ahead = slice(HALO + 1, HALO + 1 + own1)
    here = slice(HALO, HALO + own1)
    behind = slice(HALO - 1, HALO - 1 + own1)
    du_even = 0.5 * (back[0][ahead] + (back[1] + back[2])[here] + (back[3] + back[4])[behind])
    du_odd = 0.5 * ((back[0] + back[1])[ahead] + (back[2] + back[3])[here] + back[4][behind])
    skip = 0.5 * dmid.astype(F32)[here, :c0]
    dg1 = jnp.zeros((1, c0), F32)
    sides = []
    for ext, du in ((xe, du_even), (xo, du_odd)):
        xs = ext[here]
        r = mean_inverse(xs)
        dn = du * gelu_slope(xs * r * gain1)
        dg1 = dg1 + jnp.sum(dn * xs * r, axis=0, keepdims=True)
        h = dn * gain1
        dx = r * h - xs * (r * r * r) * jnp.mean(h * xs, axis=-1, keepdims=True) + skip
        sides.append(dx.astype(BF16))
    weave_even = picks((2 * own1, own1), lambda i, j: i == 2 * j, 1.0)
    weave_odd = picks((2 * own1, own1), lambda i, j: i == 2 * j + 1, 1.0)
    dx_ref[0] = (dot(weave_even, sides[0]) + dot(weave_odd, sides[1])).astype(BF16)
    twin = slot(far, mid_axis, 1 - core)
    across = slot(far, 1 - mid_axis, core)
    gain_twin = remote(gbuf.at[0], gbuf.at[1], g_send.at[0], g_recv.at[0], twin)
    gain_across = remote(gbuf.at[2], gbuf.at[3], g_send.at[1], g_recv.at[1], across)

    def gain_far(d, sign):
        other = lax.rem(far + outer + sign * d, outer)
        owner = far if sign > 0 else other
        return remote(
            gbuf.at[4 + owner], gbuf.at[4 + owner], g_send.at[1 + d], g_recv.at[2 + owner], slot(other, mid_axis, core)
        )

    gbuf[0] = jnp.concatenate([dg1, dg2], axis=1)
    gain_twin.start()
    c_far()
    enc = jnp.zeros((own2, c2), F32)
    for k in range(KERNEL):
        taps = picks(
            (own2, ext1),
            lambda m, i: (i == 2 * m + k - 2 + HALO) | (i == 2 * m + k - 1 + HALO),
            0.5,
        )
        enc = enc + dot(dot(taps, u2).astype(BF16), w2_ref[:, k * c2 : (k + 1) * c2])
    halves = picks((own2, ext1), lambda m, i: (i == 2 * m + HALO) | (i == 2 * m + 1 + HALO), 0.5)
    pooled = dot(halves, mid)
    if c2 > c1:
        pooled = jnp.concatenate([pooled, jnp.zeros((own2, c2 - c1), F32)], axis=1)
    enc_ref[0] = (enc + pooled).astype(BF16)

    gain_twin.wait_recv()
    gbuf[2] = gbuf[0] + gbuf[1]
    gain_across.start()
    c_across()

    def taps_of(read, rows, length):
        group = 128 // length
        lane = lax.broadcasted_iota(jnp.int32, (rows, 128), 1)
        evens, odds = [], []
        for s in range(0, n, group):
            even = odd = jnp.zeros((rows, 128), F32)
            for g in range(group):
                block = read(s + g)
                chosen = (lane >= g * length) & (lane < (g + 1) * length)
                shift = g * length
                even = jnp.where(chosen, pltpu.roll(block, shift, 1) if shift else block, even)
                shift = (g * length - length) % 128
                odd = jnp.where(chosen, pltpu.roll(block, shift, 1) if shift else block, odd)
            evens.append(even)
            odds.append(odd)
        even = jnp.concatenate(evens, axis=1)
        odd = jnp.concatenate(odds, axis=1)
        total = n * length
        lanes = lax.broadcasted_iota(jnp.int32, (rows, total), 1)

        def later(v):
            return jnp.where(lanes == 0, 0.0, pltpu.roll(v, 1, 1))

        def sooner(v):
            return jnp.where(lanes == total - 1, 0.0, pltpu.roll(v, total - 1, 1))

        pair = 0.5 * (even + odd)
        blocks = [later(pair), 0.5 * (later(odd) + even), pair, 0.5 * (odd + sooner(even)), sooner(pair)]
        return jnp.concatenate(blocks, axis=0).astype(BF16)

    def padded(block, rows):
        if rows == block.shape[0]:
            return block
        return jnp.concatenate([block, jnp.zeros((rows - block.shape[0], 128), F32)], axis=0)

    def unfolded(s):
        block = arecv2[s].astype(F32)
        return padded(jnp.concatenate([block, pltpu.roll(block, 64, 1)], axis=0), pad2)

    lax.fori_loop(1, n, a_done, 0)
    stack1 = taps_of(lambda s: padded(arecv1[s].astype(F32), pad1), pad1, own1)
    gain_across.wait_recv()
    gbuf[4 + far] = gbuf[2] + gbuf[3]
    for d in range(1, outer):
        gain_far(d, 1).start()
    u_finish()
    lax.fori_loop(1, n, b_done, 0)
    stack2 = taps_of(unfolded, pad2, own2)
    grad2 = dot(stack2, ubuf[...].reshape(n * own2, c2))
    for k in range(KERNEL):
        dw2_ref[:, k * c2 : (k + 1) * c2] = grad2[k * pad2 : k * pad2 + rows2]
    for d in range(1, outer):
        gain_far(d, -1).wait_recv()
    gains = jnp.sum(gbuf[4 : 4 + outer], axis=0)
    dg1_ref[...] = gains[:, :c0].reshape(c0)
    dg2_ref[...] = gains[:, c0:].reshape(c1)
    c_finish()
    grad1 = dot(stack1, cbuf[...].reshape(n * own1, c1))
    for k in range(KERNEL):
        dw1_ref[:, k * c1 : (k + 1) * c1] = grad1[k * pad1 : k * pad1 + rows1]

    @pl.when(me < n - 1)
    def _():
        x_to_right.wait_send()
        u_to_right.wait_send()

    @pl.when(me > 0)
    def _():
        x_to_left.wait_send()
        u_to_left.wait_send()

    u_drain()
    c_drain()
    gain_twin.wait_send()
    gain_across.wait_send()
    for d in range(1, outer):
        gain_far(d, 1).wait_send()

    def drain(d, _):
        a_copy(d).wait_send()
        b_copy(d).wait_send()
        return 0

    lax.fori_loop(1, n, drain, 0)


def place_results(*refs):
    count = len(refs) // 2
    sems = refs[-1]
    copies = [pltpu.make_async_copy(refs[i], refs[count + i], sems.at[i]) for i in range(count)]
    for copy in copies:
        copy.start()
    for copy in copies:
        copy.wait()


def shards(features, gain_first, weight_first, gain_second, weight_second, upstream):
    n = lax.axis_size("seq")
    length, c0 = features.shape[1:]
    own2, c2 = upstream.shape[1:]
    c1 = weight_second.shape[0]
    own1 = length // 2
    dma = pltpu.SemaphoreType.DMA
    vmem = pl.BlockSpec(memory_space=pltpu.VMEM)
    hbm = pl.BlockSpec(memory_space=pl.ANY)
    results = pl.pallas_call(
        functools.partial(kernel, n),
        out_shape=(
            jax.ShapeDtypeStruct((1, own2, c2), BF16),
            jax.ShapeDtypeStruct((1, length, c0), BF16),
            jax.ShapeDtypeStruct((c0 // n, KERNEL * c1), F32),
            jax.ShapeDtypeStruct((c1 // n, KERNEL * c2), F32),
            jax.ShapeDtypeStruct((c0,), F32),
            jax.ShapeDtypeStruct((c1,), F32),
        ),
        in_specs=[vmem, vmem, hbm, vmem, hbm, vmem],
        out_specs=(vmem,) * 6,
        scratch_shapes=[
            pltpu.VMEM(weight_first.shape, BF16),
            pltpu.VMEM(weight_second.shape, BF16),
            pltpu.VMEM((16, c0), BF16),
            pltpu.VMEM((16, c0), BF16),
            pltpu.VMEM((16, c2), BF16),
            pltpu.VMEM((16, c2), BF16),
            pltpu.VMEM((n, own1, c1), BF16),
            pltpu.VMEM((n, own2, c2), BF16),
            pltpu.VMEM((n, c0 // n, 128), BF16),
            pltpu.VMEM((n, c0 // n, 128), BF16),
            pltpu.VMEM((n, c1 // n // 2, 128), BF16),
            pltpu.VMEM((n, c1 // n // 2, 128), BF16),
            pltpu.VMEM((4 + n // 4, 1, c0 + c1), F32),
            dma((2,)), dma((4,)), dma((4,)),
            dma((n,)), dma((n,)), dma((n,)), dma((n,)), dma((n,)), dma((n,)), dma((n,)), dma((n,)),
            dma((1 + n // 4,)), dma((2 + n // 4,)),
        ],
        compiler_params=pltpu.CompilerParams(
            collective_id=0, has_side_effects=True, vmem_limit_bytes=56 * 1024 * 1024
        ),
    )(
        features,
        gain_first,
        weight_first,
        gain_second,
        weight_second,
        upstream,
    )
    return pl.pallas_call(
        place_results,
        out_shape=tuple(jax.ShapeDtypeStruct(r.shape, r.dtype) for r in results),
        in_specs=[vmem] * len(results),
        out_specs=(hbm,) * len(results),
        scratch_shapes=[dma((len(results),))],
    )(*results)


def solution(mesh):
    placed = (P("groups", "seq", None), P(), P(), P(), P(), P("groups", "seq", None))
    return jax.shard_map(
        shards,
        mesh=mesh,
        in_specs=placed,
        out_specs=(
            P("groups", "seq", None),
            P("groups", "seq", None),
            P(("groups", "seq"), None),
            P(("groups", "seq"), None),
            P("groups"),
            P("groups"),
        ),
        check_vma=False,
    )
```

```python
import functools
import jax
import jax.numpy as jnp
from jax import lax
from jax.experimental import pallas as pl
from jax.experimental.pallas import tpu as pltpu
from jax.sharding import PartitionSpec as P

KERNEL = 5
GELU_A = 0.7978845608028654
GELU_B = 0.044715
HALO = 8
F32 = jnp.float32
BF16 = jnp.bfloat16


def round16(rows):
    return (rows + 15) // 16 * 16


def dot(a, b):
    return jnp.dot(a, b, preferred_element_type=F32)


def dot_t(a, b):
    return lax.dot_general(a, b, (((1,), (1,)), ((), ())), preferred_element_type=F32)


def mean_inverse(x):
    return lax.rsqrt(jnp.mean(x * x, axis=-1, keepdims=True) + 1e-06)


def gelu(x):
    return 0.5 * x * (1.0 + jnp.tanh(GELU_A * (x + GELU_B * x * x * x)))


def gelu_slope(x):
    t = jnp.tanh(GELU_A * (x + GELU_B * x * x * x))
    return 0.5 * (1.0 + t) + 0.5 * x * (1.0 - t * t) * GELU_A * (1.0 + 3.0 * GELU_B * x * x)


def picks(shape, test, value):
    row = lax.broadcasted_iota(jnp.int32, shape, 0)
    col = lax.broadcasted_iota(jnp.int32, shape, 1)
    return jnp.where(test(row, col), value, 0.0).astype(BF16)


def kernel(
    n, x_ref, g1_ref, w1_hbm, g2_ref, w2_hbm, up_ref,
    enc_ref, dx_ref, dw1_ref, dw2_ref, dg1_ref, dg2_ref,
    w1_ref, w2_ref, xl_ref, xr_ref, ul_ref, ur_ref,
    cbuf, ubuf, asend1, arecv1, asend2, arecv2, gbuf,
    w_sem, halo_send, halo_recv, c_send, c_recv, u_send, u_recv, a_send, a_recv, b_send, b_recv, g_send, g_recv,
):
    me = lax.axis_index("seq")
    own1, c0 = x_ref.shape[1] // 2, x_ref.shape[2]
    own2, c2 = up_ref.shape[1:]
    c1 = g2_ref.shape[0]
    ext1, ext2 = own1 + 2 * HALO, own2 + 2 * HALO
    rows1, rows2 = c0 // n, c1 // n
    pad1, pad2 = round16(rows1), round16(rows2)
    outer = n // 4
    core = lax.rem(me, 2)
    mid_axis = lax.rem(me // 2, 2)
    far = me // 4

    def peer_id(index):
        return {"seq": index}

    barrier = pltpu.get_barrier_semaphore()

    def greet(d, _):
        pl.semaphore_signal(barrier, inc=1, device_id=peer_id(lax.rem(me + d, n)), device_id_type=pl.DeviceIdType.MESH)
        return 0

    lax.fori_loop(1, n, greet, 0)
    w1_copy = pltpu.make_async_copy(w1_hbm, w1_ref, w_sem.at[0])
    w2_copy = pltpu.make_async_copy(w2_hbm, w2_ref, w_sem.at[1])
    w2_copy.start()
    w1_copy.start()
    ubuf[me] = up_ref[0]
    pl.semaphore_wait(barrier, n - 1)

    def remote(src, dst, send, recv, index):
        return pltpu.make_async_remote_copy(
            src_ref=src, dst_ref=dst, send_sem=send, recv_sem=recv,
            device_id=peer_id(index), device_id_type=pl.DeviceIdType.MESH,
        )

    left, right = lax.rem(me + n - 1, n), lax.rem(me + 1, n)
    x_to_right = remote(x_ref.at[0, pl.ds(2 * own1 - 16, 16)], xl_ref, halo_send.at[0], halo_recv.at[0], right)
    x_to_left = remote(x_ref.at[0, pl.ds(0, 16)], xr_ref, halo_send.at[1], halo_recv.at[1], left)
    u_to_right = remote(up_ref.at[0, pl.ds(own2 - 16, 16)], ul_ref, halo_send.at[2], halo_recv.at[2], right)
    u_to_left = remote(up_ref.at[0, pl.ds(0, 16)], ur_ref, halo_send.at[3], halo_recv.at[3], left)

    @pl.when(me < n - 1)
    def _():
        x_to_right.start()
        u_to_right.start()

    @pl.when(me > 0)
    def _():
        x_to_left.start()
        u_to_left.start()

    def slot(f, m, c):
        return (f * 2 + m) * 2 + c

    def gather_parts(buf, send, recv):
        def push(owner, target, k):
            return remote(buf.at[owner], buf.at[owner], send.at[k], recv.at[owner], target)

        def arrive(owner):
            push(owner, right, 0).wait_recv()

        nearest = sorted(range(1, outer), key=lambda d: min(d, outer - d))
        along = [lax.rem(far + d, outer) for d in range(outer)]
        back = [lax.rem(far + outer - d, outer) for d in range(outer)]
        across = slot(far, 1 - mid_axis, core)
        twin = slot(far, mid_axis, 1 - core)

        def begin():
            push(me, across, 0).start()
            for d in nearest:
                push(me, slot(along[d], mid_axis, core), d).start()
            push(me, twin, outer).start()

        def relay_far():
            for d in nearest:
                owner = slot(back[d], mid_axis, core)
                arrive(owner)
                push(owner, across, outer + d).start()
                push(owner, twin, 2 * outer - 1 + d).start()

        def relay_across():
            for d in [0] + nearest:
                owner = slot(back[d], 1 - mid_axis, core)
                arrive(owner)
                push(owner, twin, 3 * outer - 1 + d).start()

        def finish():
            for d in range(outer):
                for m in range(2):
                    arrive(slot(back[d], m, 1 - core))

        def drain():
            for k in range(n - 1):
                push(me, right, k).wait_send()

        return begin, relay_far, relay_across, finish, drain

    u_begin, u_far, u_across, u_finish, u_drain = gather_parts(ubuf, u_send, u_recv)
    c_begin, c_far, c_across, c_finish, c_drain = gather_parts(cbuf, c_send, c_recv)
    u_begin()

    @pl.when(me == 0)
    def _():
        xl_ref[...] = jnp.zeros_like(xl_ref)
        ul_ref[...] = jnp.zeros_like(ul_ref)

    @pl.when(me == n - 1)
    def _():
        xr_ref[...] = jnp.zeros_like(xr_ref)
        ur_ref[...] = jnp.zeros_like(ur_ref)

    @pl.when(me > 0)
    def _():
        x_to_right.wait_recv()
        u_to_right.wait_recv()

    @pl.when(me < n - 1)
    def _():
        x_to_left.wait_recv()
        u_to_left.wait_recv()

    gain1, gain2 = g1_ref[...].reshape(1, c0), g2_ref[...].reshape(1, c1)
    x = jnp.concatenate([xl_ref[...], x_ref[0], xr_ref[...]], axis=0)

    def activate(part):
        r = mean_inverse(part)
        return r, gelu(part * r * gain1).astype(BF16).astype(F32)

    xe = dot(picks((ext1, 2 * ext1), lambda j, i: i == 2 * j, 1.0), x)
    xo = dot(picks((ext1, 2 * ext1), lambda j, i: i == 2 * j + 1, 1.0), x)
    _, ue = activate(xe)
    _, uo = activate(xo)
    pairs = 0.5 * (ue + uo)
    cross = 0.5 * (pltpu.roll(uo, 1, 0) + ue)
    columns1 = jnp.concatenate([ue[HALO : HALO + own1], uo[HALO : HALO + own1]], axis=0).T
    for s in range(n):
        asend1[s] = columns1[s * rows1 : (s + 1) * rows1].astype(BF16)
    arecv1[me] = asend1[me]

    def exchange(sent, received, send, recv):
        def copy(d):
            target = lax.rem(me + d, n)
            return remote(sent.at[target], received.at[me], send.at[d], recv.at[me], target)

        def start(d, _):
            copy(d).start()
            return 0

        def arrive(d, _):
            source = lax.rem(me + n - d, n)
            remote(sent.at[source], received.at[source], send.at[d], recv.at[source], source).wait_recv()
            return 0

        return copy, start, arrive

    a_copy, a_start, a_done = exchange(asend1, arecv1, a_send, a_recv)
    b_copy, b_start, b_done = exchange(asend2, arecv2, b_send, b_recv)
    lax.fori_loop(1, n, a_start, 0)
    w2_copy.wait()
    up = jnp.concatenate(
        [ul_ref[...].astype(F32)[16 - HALO :], up_ref[0].astype(F32), ur_ref[...].astype(F32)[:HALO]], axis=0
    ).astype(BF16)
    du2 = jnp.zeros((ext1, c1), F32)
    spread = None
    for k in range(KERNEL):
        pick = picks(
            (ext1, ext2),
            lambda i, r: (2 * r == i + HALO + 2 - k) | (2 * r + 1 == i + HALO + 2 - k),
            0.5,
        )
        part = dot(pick, up)
        if k == KERNEL // 2:
            spread = part
        du2 = du2 + dot_t(part.astype(BF16), w2_ref[:, k * c2 : (k + 1) * c2])

    w1_copy.wait()
    sources = [pltpu.roll(pairs, 1, 0), cross, pairs, pltpu.roll(cross, ext1 - 1, 0), pltpu.roll(pairs, ext1 - 1, 0)]
    conv = jnp.zeros((ext1, c1), F32)
    for k in range(KERNEL):
        conv = conv + dot(sources[k].astype(BF16), w1_ref[:, k * c1 : (k + 1) * c1])
    held = 0.5 * (xe + xo)
    if c1 > c0:
        held = jnp.concatenate([held, jnp.zeros((ext1, c1 - c0), F32)], axis=1)
    place = me * own1 - HALO + lax.broadcasted_iota(jnp.int32, (ext1, 1), 0)
    inside = (place >= 0) & (place < n * own1)
    mid = jnp.where(inside, conv + held, 0.0).astype(BF16)
    midf = mid.astype(F32)
    r2 = mean_inverse(midf)
    n2 = midf * r2 * gain2
    u2 = gelu(n2).astype(BF16)
    dn2 = du2 * gelu_slope(n2)
    terms2 = dn2 * midf * r2
    dg2 = jnp.sum(terms2[HALO : HALO + own1], axis=0, keepdims=True)
    h2 = dn2 * gain2
    dmid = r2 * h2 - midf * (r2 * r2 * r2) * jnp.mean(h2 * midf, axis=-1, keepdims=True) + spread
    dmid = jnp.where(inside, dmid, 0.0)
    cbuf[me] = dmid[HALO : HALO + own1].astype(BF16)
    dmid = dmid.astype(BF16)
    c_begin()

    order = picks(
        (128, ext1),
        lambda t, i: ((t % 64 < own2) & (i == 2 * (t % 64) + HALO))
        | ((t % 64 >= own2) & (i == 2 * (t % 64 - own2) + HALO + 1)),
        1.0,
    )
    columns2 = dot(order, u2).T
    low = lax.broadcasted_iota(jnp.int32, (rows2 // 2, 128), 1) < 64
    for s in range(n):
        top = columns2[s * rows2 : s * rows2 + rows2 // 2]
        bottom = columns2[s * rows2 + rows2 // 2 : (s + 1) * rows2]
        asend2[s] = jnp.where(low, top, bottom).astype(BF16)
    arecv2[me] = asend2[me]
    u_far()

    back = [dot_t(dmid, w1_ref[:, k * c1 : (k + 1) * c1]) for k in range(KERNEL)]
    ahead = slice(HALO + 1, HALO + 1 + own1)
    here = slice(HALO, HALO + own1)
    behind = slice(HALO - 1, HALO - 1 + own1)
    du_even = 0.5 * (back[0][ahead] + (back[1] + back[2])[here] + (back[3] + back[4])[behind])
    du_odd = 0.5 * ((back[0] + back[1])[ahead] + (back[2] + back[3])[here] + back[4][behind])
    skip = 0.5 * dmid.astype(F32)[here, :c0]
    dg1 = jnp.zeros((1, c0), F32)
    sides = []
    for ext, du in ((xe, du_even), (xo, du_odd)):
        xs = ext[here]
        r = mean_inverse(xs)
        dn = du * gelu_slope(xs * r * gain1)
        dg1 = dg1 + jnp.sum(dn * xs * r, axis=0, keepdims=True)
        h = dn * gain1
        dx = r * h - xs * (r * r * r) * jnp.mean(h * xs, axis=-1, keepdims=True) + skip
        sides.append(dx.astype(BF16))
    weave_even = picks((2 * own1, own1), lambda i, j: i == 2 * j, 1.0)
    weave_odd = picks((2 * own1, own1), lambda i, j: i == 2 * j + 1, 1.0)
    dx_ref[0] = (dot(weave_even, sides[0]) + dot(weave_odd, sides[1])).astype(BF16)
    twin = slot(far, mid_axis, 1 - core)
    across = slot(far, 1 - mid_axis, core)
    gain_twin = remote(gbuf.at[0], gbuf.at[1], g_send.at[0], g_recv.at[0], twin)
    gain_across = remote(gbuf.at[2], gbuf.at[3], g_send.at[1], g_recv.at[1], across)

    def gain_far(d, sign):
        other = lax.rem(far + outer + sign * d, outer)
        owner = far if sign > 0 else other
        return remote(
            gbuf.at[4 + owner], gbuf.at[4 + owner], g_send.at[1 + d], g_recv.at[2 + owner], slot(other, mid_axis, core)
        )

    gbuf[0] = jnp.concatenate([dg1, dg2], axis=1)
    gain_twin.start()
    c_far()
    lax.fori_loop(1, n, b_start, 0)
    gain_twin.wait_recv()
    gbuf[2] = gbuf[0] + gbuf[1]
    gain_across.start()
    u_across()
    enc = jnp.zeros((own2, c2), F32)
    for k in range(KERNEL):
        taps = picks(
            (own2, ext1),
            lambda m, i: (i == 2 * m + k - 2 + HALO) | (i == 2 * m + k - 1 + HALO),
            0.5,
        )
        enc = enc + dot(dot(taps, u2).astype(BF16), w2_ref[:, k * c2 : (k + 1) * c2])
    halves = picks((own2, ext1), lambda m, i: (i == 2 * m + HALO) | (i == 2 * m + 1 + HALO), 0.5)
    pooled = dot(halves, mid)
    if c2 > c1:
        pooled = jnp.concatenate([pooled, jnp.zeros((own2, c2 - c1), F32)], axis=1)
    enc_ref[0] = (enc + pooled).astype(BF16)

    gain_across.wait_recv()
    gbuf[4 + far] = gbuf[2] + gbuf[3]
    for d in range(1, outer):
        gain_far(d, 1).start()
    c_across()

    def taps_of(read, rows, length):
        group = 128 // length
        lane = lax.broadcasted_iota(jnp.int32, (rows, 128), 1)
        evens, odds = [], []
        for s in range(0, n, group):
            even = odd = jnp.zeros((rows, 128), F32)
            for g in range(group):
                block = read(s + g)
                chosen = (lane >= g * length) & (lane < (g + 1) * length)
                shift = g * length
                even = jnp.where(chosen, pltpu.roll(block, shift, 1) if shift else block, even)
                shift = (g * length - length) % 128
                odd = jnp.where(chosen, pltpu.roll(block, shift, 1) if shift else block, odd)
            evens.append(even)
            odds.append(odd)
        even = jnp.concatenate(evens, axis=1)
        odd = jnp.concatenate(odds, axis=1)
        total = n * length
        lanes = lax.broadcasted_iota(jnp.int32, (rows, total), 1)

        def later(v):
            return jnp.where(lanes == 0, 0.0, pltpu.roll(v, 1, 1))

        def sooner(v):
            return jnp.where(lanes == total - 1, 0.0, pltpu.roll(v, total - 1, 1))

        pair = 0.5 * (even + odd)
        blocks = [later(pair), 0.5 * (later(odd) + even), pair, 0.5 * (odd + sooner(even)), sooner(pair)]
        return jnp.concatenate(blocks, axis=0).astype(BF16)

    def padded(block, rows):
        if rows == block.shape[0]:
            return block
        return jnp.concatenate([block, jnp.zeros((rows - block.shape[0], 128), F32)], axis=0)

    def unfolded(s):
        block = arecv2[s].astype(F32)
        return padded(jnp.concatenate([block, pltpu.roll(block, 64, 1)], axis=0), pad2)

    lax.fori_loop(1, n, a_done, 0)
    stack1 = taps_of(lambda s: padded(arecv1[s].astype(F32), pad1), pad1, own1)
    u_finish()
    lax.fori_loop(1, n, b_done, 0)
    stack2 = taps_of(unfolded, pad2, own2)
    grad2 = dot(stack2, ubuf[...].reshape(n * own2, c2))
    for k in range(KERNEL):
        dw2_ref[:, k * c2 : (k + 1) * c2] = grad2[k * pad2 : k * pad2 + rows2]
    for d in range(1, outer):
        gain_far(d, -1).wait_recv()
    gains = jnp.sum(gbuf[4 : 4 + outer], axis=0)
    dg1_ref[...] = gains[:, :c0].reshape(c0)
    dg2_ref[...] = gains[:, c0:].reshape(c1)
    c_finish()
    grad1 = dot(stack1, cbuf[...].reshape(n * own1, c1))
    for k in range(KERNEL):
        dw1_ref[:, k * c1 : (k + 1) * c1] = grad1[k * pad1 : k * pad1 + rows1]

    @pl.when(me < n - 1)
    def _():
        x_to_right.wait_send()
        u_to_right.wait_send()

    @pl.when(me > 0)
    def _():
        x_to_left.wait_send()
        u_to_left.wait_send()

    u_drain()
    c_drain()
    gain_twin.wait_send()
    gain_across.wait_send()
    for d in range(1, outer):
        gain_far(d, 1).wait_send()

    def drain(d, _):
        a_copy(d).wait_send()
        b_copy(d).wait_send()
        return 0

    lax.fori_loop(1, n, drain, 0)


def place_results(*refs):
    count = len(refs) // 2
    sems = refs[-1]
    copies = [pltpu.make_async_copy(refs[i], refs[count + i], sems.at[i]) for i in range(count)]
    for copy in copies:
        copy.start()
    for copy in copies:
        copy.wait()


def shards(features, gain_first, weight_first, gain_second, weight_second, upstream):
    n = lax.axis_size("seq")
    length, c0 = features.shape[1:]
    own2, c2 = upstream.shape[1:]
    c1 = weight_second.shape[0]
    own1 = length // 2
    dma = pltpu.SemaphoreType.DMA
    vmem = pl.BlockSpec(memory_space=pltpu.VMEM)
    hbm = pl.BlockSpec(memory_space=pl.ANY)
    results = pl.pallas_call(
        functools.partial(kernel, n),
        out_shape=(
            jax.ShapeDtypeStruct((1, own2, c2), BF16),
            jax.ShapeDtypeStruct((1, length, c0), BF16),
            jax.ShapeDtypeStruct((c0 // n, KERNEL * c1), F32),
            jax.ShapeDtypeStruct((c1 // n, KERNEL * c2), F32),
            jax.ShapeDtypeStruct((c0,), F32),
            jax.ShapeDtypeStruct((c1,), F32),
        ),
        in_specs=[vmem, vmem, hbm, vmem, hbm, vmem],
        out_specs=(vmem,) * 6,
        scratch_shapes=[
            pltpu.VMEM(weight_first.shape, BF16),
            pltpu.VMEM(weight_second.shape, BF16),
            pltpu.VMEM((16, c0), BF16),
            pltpu.VMEM((16, c0), BF16),
            pltpu.VMEM((16, c2), BF16),
            pltpu.VMEM((16, c2), BF16),
            pltpu.VMEM((n, own1, c1), BF16),
            pltpu.VMEM((n, own2, c2), BF16),
            pltpu.VMEM((n, c0 // n, 128), BF16),
            pltpu.VMEM((n, c0 // n, 128), BF16),
            pltpu.VMEM((n, c1 // n // 2, 128), BF16),
            pltpu.VMEM((n, c1 // n // 2, 128), BF16),
            pltpu.VMEM((4 + n // 4, 1, c0 + c1), F32),
            dma((2,)), dma((4,)), dma((4,)),
            dma((n,)), dma((n,)), dma((n,)), dma((n,)), dma((n,)), dma((n,)), dma((n,)), dma((n,)),
            dma((1 + n // 4,)), dma((2 + n // 4,)),
        ],
        compiler_params=pltpu.CompilerParams(
            collective_id=0, has_side_effects=True, vmem_limit_bytes=56 * 1024 * 1024
        ),
    )(
        features,
        gain_first,
        weight_first,
        gain_second,
        weight_second,
        upstream,
    )
    return pl.pallas_call(
        place_results,
        out_shape=tuple(jax.ShapeDtypeStruct(r.shape, r.dtype) for r in results),
        in_specs=[vmem] * len(results),
        out_specs=(hbm,) * len(results),
        scratch_shapes=[dma((len(results),))],
    )(*results)


def solution(mesh):
    placed = (P("groups", "seq", None), P(), P(), P(), P(), P("groups", "seq", None))
    return jax.shard_map(
        shards,
        mesh=mesh,
        in_specs=placed,
        out_specs=(
            P("groups", "seq", None),
            P("groups", "seq", None),
            P(("groups", "seq"), None),
            P(("groups", "seq"), None),
            P("groups"),
            P("groups"),
        ),
        check_vma=False,
    )
```
